32 devices in a mesh: group: 2 (over x), seq: 16 (over z, y, core).
Axes of the slice: x: 2, y: 2, z: 4, core: 2. Of those that a mesh axis runs over, the one named last changes fastest.
Arguments:
- x_rows: bfloat16 [32, 8192], P('group', 'seq'), parts along dimension 0, may hold values from -0.59765625 to 0.59765625
- attn_gain: bfloat16 [8192], replicated, may hold values from 0.5 to 1.5
- q_weight: bfloat16 [8192, 8192], P(None, 'seq'), may hold values from -0.0625 to 0.0625
- o_weight: bfloat16 [8192, 8192], P('seq'), may hold values from -0.0625 to 0.0625
- mlp_gain: bfloat16 [8192], replicated, may hold values from 0.5 to 1.5
- gate_weight: bfloat16 [8192, 14336], P(None, 'seq'), may hold values from -0.0625 to 0.0625
- up_weight: bfloat16 [8192, 14336], P(None, 'seq'), may hold values from -0.0625 to 0.0625
- down_weight: bfloat16 [14336, 8192], P('seq'), may hold values from -0.046875 to 0.046875
- kv_cache: bfloat16 [2, 4096, 1024], P(None, ('group', 'seq')), parts along dimension 1, may hold values from -250 to 250, as said below
- block_mask: int32 [32, 8, 16], P('group', None, 'seq'), parts along dimension 0, may hold values from 0 to 1, as said below
Outputs:
- y_rows: bfloat16 [32, 8192], P('group', 'seq'), parts along dimension 0
The draws below stay inside these ranges and needn't reach their ends.
There are 2 independent parts, one for each index of `group`. The reference program is written for one: setup_inputs(seed, part) draws one part's arguments, and reference() takes and returns one part's arrays. A program takes and returns all parts, laid end to end along the dimension named above; an argument that names none is the same for every part. Nothing has to cross between parts.
Inputs may be any that keep to these rules, and one draw needn't show every extreme that they name: `kv_cache`: document keys and values; they differ from document to document. `block_mask`: 1 where the row may attend to that block of 128 document tokens for that key-value head, else 0; the document's last block is 1 for every row and key-value head.
All inputs are finite; a program needn't handle non-finite values.
Results may differ from the reference program's by a relative error of at most 0.013.
The reference program's roundings to bfloat16 on the way (of `normed`, `queries`, `attended`, `stream`, `normed_two` and `hidden`) count: a program that leaves them out, or rounds other values in their place, can miss the bound.
Values may be sent and summed in bfloat16 or wider, within the bound.
A program may use at most 192 MiB of HBM per device.

```python
import jax
import jax.numpy as jnp
from jax import lax

D = 8192
HEADS = 64
KV_HEADS = 8
HEAD_DIM = 128
FF_WIN = 14336
BLOCK = 128
ROWS = 16
KV_DEV = 128
DOC = 2048
NBLK = 16
N_SEQ = 16


def draw_kv_cache(key, part):
    width = KV_HEADS * HEAD_DIM
    keys = 1.5 * jnp.clip(jax.random.normal(jax.random.fold_in(key, 21), (DOC, width), jnp.float32), -4.0, 4.0)
    values = 4.0 * jnp.clip(jax.random.normal(jax.random.fold_in(key, 22), (DOC, width), jnp.float32), -4.0, 4.0)
    return jnp.stack([keys, values]).astype(jnp.bfloat16)


def draw_block_mask(key, part):
    position = jnp.arange(NBLK, dtype=jnp.int32)
    limit = 150 + 800 * position * position // (NBLK * NBLK)
    rolled = jax.random.randint(jax.random.fold_in(key, 31), (ROWS, KV_HEADS, NBLK), 0, 1000, jnp.int32)
    drawn = (rolled < limit[None, None, :]).astype(jnp.int32)
    last = (position == NBLK - 1)[None, None, :]
    return jnp.where(last, 1, drawn).astype(jnp.int32)


def levels(rng, extent, shards, low, high):
    loudness, own = 1.0, jax.random.fold_in(rng, 6)
    for axis_at, parts in shards:
        draws = jnp.exp(jax.random.uniform(jax.random.fold_in(own, axis_at), (parts,), jnp.float32, low / len(shards), high / len(shards)))
        loudness = loudness * jnp.repeat(draws, extent[axis_at] // parts).reshape([-1 if axis == axis_at else 1 for axis in range(len(extent))])
    return loudness


def gaussian(rng, dims, deviation, bound, split=(), kind=jnp.bfloat16):
    level = levels(rng, dims, split, -0.22, 0.18) if split else 1.0
    result = jax.random.normal(rng, dims, jnp.float32) * deviation * level
    return jnp.minimum(jnp.maximum(result, -bound), bound).astype(kind)


def setup_inputs(seed: int = 0, part: int = 0) -> dict:
    key_of = jax.random.split(jax.random.key(seed), 11)
    part_splits = jax.random.split(jax.random.fold_in(key_of[10], part), 11)
    return {
        "x_rows": gaussian(part_splits[0], (ROWS, D), 0.1, 0.59765625, ((1, 16),)),
        "attn_gain": jnp.clip(1.0 + 0.1 * jax.random.normal(key_of[1], (D,), jnp.float32), 0.5, 1.5).astype(jnp.bfloat16),
        "q_weight": gaussian(key_of[2], (D, HEADS * HEAD_DIM), D ** -0.5, 0.0625, ((1, 16),)),
        "o_weight": gaussian(key_of[3], (HEADS * HEAD_DIM, D), (HEADS * HEAD_DIM) ** -0.5, 0.0625, ((0, 16),)),
        "mlp_gain": jnp.clip(1.0 + 0.1 * jax.random.normal(key_of[4], (D,), jnp.float32), 0.5, 1.5).astype(jnp.bfloat16),
        "gate_weight": gaussian(key_of[5], (D, FF_WIN), D ** -0.5, 0.0625, ((1, 16),)),
        "up_weight": gaussian(key_of[6], (D, FF_WIN), D ** -0.5, 0.0625, ((1, 16),)),
        "down_weight": gaussian(key_of[7], (FF_WIN, D), FF_WIN ** -0.5, 0.046875, ((0, 16),)),
        "kv_cache": draw_kv_cache(jax.random.fold_in(jax.random.fold_in(key_of[10], part), 71), part),
        "block_mask": draw_block_mask(jax.random.fold_in(jax.random.fold_in(key_of[10], part), 71), part),
    }


eps = 1e-05
floor_score = -1e+30

def rms_norm(values, gain):
    wide = values.astype(jnp.float32)
    inverse = lax.rsqrt(lax.optimization_barrier(jnp.mean(wide * wide, axis=-1, keepdims=True)) + eps)
    return (wide * inverse * gain.astype(jnp.float32)).astype(jnp.bfloat16)

def reference(x_rows, attn_gain, q_weight, o_weight, mlp_gain, gate_weight, up_weight, down_weight, kv_cache, block_mask):
    rows = x_rows.shape[0]
    group = HEADS // KV_HEADS
    spans = KV_DEV // BLOCK
    scale = 1.0 / HEAD_DIM ** 0.5
    normed = rms_norm(x_rows, attn_gain)
    queries = jnp.dot(normed, q_weight, preferred_element_type=jnp.float32).astype(jnp.bfloat16)
    query_wide = queries.reshape(rows, KV_HEADS, group, HEAD_DIM).astype(jnp.float32)
    doc_keys = kv_cache[0]
    doc_values = kv_cache[1]

    def one_span(carry, index):
        top, total, accum = carry
        start = (index * KV_DEV).astype(jnp.int32)
        span_keys = lax.dynamic_slice_in_dim(doc_keys, start, KV_DEV, 0).reshape(KV_DEV, KV_HEADS, HEAD_DIM).astype(jnp.float32)
        span_values = lax.dynamic_slice_in_dim(doc_values, start, KV_DEV, 0).reshape(KV_DEV, KV_HEADS, HEAD_DIM).astype(jnp.float32)
        span_mask = lax.dynamic_slice_in_dim(block_mask, (index * spans).astype(jnp.int32), spans, 2)
        scores = jnp.einsum('rghd,kgd->rghk', query_wide, span_keys) * scale
        scores = scores.reshape(rows, KV_HEADS, group, spans, BLOCK)
        live = (span_mask == 1)[:, :, None, :, None]
        masked = jnp.where(live, scores, floor_score)
        local_top = lax.optimization_barrier(jnp.max(masked, axis=(3, 4)))
        weights = jnp.where(live, jnp.exp(masked - local_top[..., None, None]), 0.0)
        local_total = lax.optimization_barrier(jnp.sum(weights, axis=(3, 4)))
        rounded = lax.optimization_barrier(weights.astype(jnp.bfloat16)).astype(jnp.float32)
        rounded = rounded.reshape(rows, KV_HEADS, group, KV_DEV)
        local_accum = jnp.einsum('rghk,kgd->rghd', rounded, span_values)
        new_top = jnp.maximum(top, local_top)
        old_factor = jnp.exp(top - new_top)
        new_factor = jnp.exp(local_top - new_top)
        total = total * old_factor + local_total * new_factor
        accum = accum * old_factor[..., None] + local_accum * new_factor[..., None]
        return ((new_top, total, accum), None)
    init = (jnp.full((rows, KV_HEADS, group), floor_score, jnp.float32), jnp.zeros((rows, KV_HEADS, group), jnp.float32), jnp.zeros((rows, KV_HEADS, group, HEAD_DIM), jnp.float32))
    (top, total, accum), _ = lax.scan(one_span, init, jnp.arange(N_SEQ, dtype=jnp.int32))
    attended = accum / total[..., None]
    attended = attended.reshape(rows, HEADS * HEAD_DIM).astype(jnp.bfloat16)
    stream = (x_rows.astype(jnp.float32) + jnp.dot(attended, o_weight, preferred_element_type=jnp.float32)).astype(jnp.bfloat16)
    normed_two = rms_norm(stream, mlp_gain)
    gate = jnp.dot(normed_two, gate_weight, preferred_element_type=jnp.float32)
    upward = jnp.dot(normed_two, up_weight, preferred_element_type=jnp.float32)
    hidden = (jax.nn.silu(gate) * upward).astype(jnp.bfloat16)
    return (stream.astype(jnp.float32) + jnp.dot(hidden, down_weight, preferred_element_type=jnp.float32)).astype(jnp.bfloat16)
```

```python
import functools

import jax
import jax.numpy as jnp
from jax import lax
from jax.experimental import pallas as pl
from jax.experimental.pallas import tpu as pltpu
from jax.sharding import PartitionSpec as P

HEADS = 64
KV_HEADS = 8
HEAD_DIM = 128
BLOCK = 128


eps = 1e-05
floor_score = -1e30


def combined_all(x, axis, combine):
    everything = jax.tree.map(lambda part: lax.all_gather(part, axis), x)
    initial = jax.tree.map(lambda part: part[0], everything)

    def turn(k, so_far):
        return combine(so_far, jax.tree.map(lambda part: part[k], everything))

    return lax.fori_loop(1, lax.axis_size(axis), turn, initial)


def rms_norm(values, gain):
    wide = values.astype(jnp.float32)
    inverse = lax.rsqrt(jnp.mean(wide * wide, axis=-1, keepdims=True) + eps)
    return (wide * inverse * gain.astype(jnp.float32)).astype(jnp.bfloat16)


def combine_states(first, second):
    top_a, total_a, accum_a = first
    top_b, total_b, accum_b = second
    top = jnp.maximum(top_a, top_b)
    factor_a = jnp.exp(top_a - top)
    factor_b = jnp.exp(top_b - top)
    return (
        top,
        total_a * factor_a + total_b * factor_b,
        accum_a * factor_a[..., None] + accum_b * factor_b[..., None],
    )


def local(
    x_rows,
    attn_gain,
    q_weight,
    o_weight,
    mlp_gain,
    gate_weight,
    up_weight,
    down_weight,
    kv_cache,
    block_mask,
):
    rows = x_rows.shape[0]
    group = HEADS // KV_HEADS
    key_len = kv_cache.shape[1]
    spans = key_len // BLOCK
    scale = 1.0 / HEAD_DIM**0.5
    whole = lax.all_gather(x_rows, "seq", axis=1, tiled=True)
    normed = rms_norm(whole, attn_gain)
    query_part = jnp.dot(normed, q_weight, preferred_element_type=jnp.float32).astype(jnp.bfloat16)
    queries = lax.all_gather(query_part, "seq", axis=1, tiled=True)
    doc_keys = kv_cache[0]
    doc_values = kv_cache[1]

    def one_group(index):
        query_group = lax.dynamic_slice_in_dim(
            queries, index * (group * HEAD_DIM), group * HEAD_DIM, 1
        ).reshape(rows, group, HEAD_DIM)
        key_group = lax.dynamic_slice_in_dim(doc_keys, index * HEAD_DIM, HEAD_DIM, 1)
        value_group = lax.dynamic_slice_in_dim(doc_values, index * HEAD_DIM, HEAD_DIM, 1)
        mask_group = lax.dynamic_slice_in_dim(block_mask, index, 1, 1)[:, 0, :]
        scores = (
            jnp.einsum("rhd,kd->rhk", query_group, key_group, preferred_element_type=jnp.float32)
            * scale
        )
        scores = scores.reshape(rows, group, spans, BLOCK)
        live = (mask_group == 1)[:, None, :, None]
        masked = jnp.where(live, scores, floor_score)
        local_top = jnp.max(masked, axis=(2, 3))
        weights = jnp.where(live, jnp.exp(masked - local_top[..., None, None]), 0.0)
        local_total = jnp.sum(weights, axis=(2, 3))
        rounded = weights.astype(jnp.bfloat16).reshape(rows, group, key_len)
        local_accum = jnp.einsum(
            "rhk,kd->rhd", rounded, value_group, preferred_element_type=jnp.float32
        )
        return (local_top, local_total, local_accum)

    tops, totals, accums = lax.map(one_group, jnp.arange(KV_HEADS, dtype=jnp.int32))
    local_top = jnp.moveaxis(tops, 0, 1)
    local_total = jnp.moveaxis(totals, 0, 1)
    local_accum = jnp.moveaxis(accums, 0, 1)
    columns = q_weight.shape[1]
    col_start = lax.axis_index("seq") * columns
    top, total, accum = combined_all((local_top, local_total, local_accum), "seq", combine_states)
    attended = accum / total[..., None]
    attended = attended.reshape(rows, HEADS * HEAD_DIM).astype(jnp.bfloat16)
    attn_cols = lax.dynamic_slice_in_dim(attended, col_start, columns, 1)
    weight_cols = o_weight
    attn_out = lax.psum_scatter(
        lax.dot_general(
            weight_cols, attn_cols, (((0,), (1,)), ((), ())), preferred_element_type=jnp.float32
        ),
        "seq",
        scatter_dimension=0,
        tiled=True,
    )
    stream = (x_rows.astype(jnp.float32) + attn_out.T).astype(jnp.bfloat16)
    stream_whole = lax.all_gather(stream, "seq", axis=1, tiled=True)
    normed_two = rms_norm(stream_whole, mlp_gain)
    gate = jnp.dot(normed_two, gate_weight, preferred_element_type=jnp.float32)
    upward = jnp.dot(normed_two, up_weight, preferred_element_type=jnp.float32)
    hidden = (jax.nn.silu(gate) * upward).astype(jnp.bfloat16)
    weight_cols = down_weight
    down_out = lax.psum_scatter(
        lax.dot_general(
            weight_cols, hidden, (((0,), (1,)), ((), ())), preferred_element_type=jnp.float32
        ),
        "seq",
        scatter_dimension=0,
        tiled=True,
    )
    return (stream.astype(jnp.float32) + down_out.T).astype(jnp.bfloat16)


FAR_FIRST = (4, 3, 5, 2, 6, 1, 7)
SCALE = 1.0 / HEAD_DIM**0.5


def layer_kernel(
    x_ref,
    attn_gain,
    q_hbm,
    o_hbm,
    mlp_gain,
    gate_hbm,
    up_hbm,
    down_hbm,
    kv_hbm,
    mask_ref,
    y_ref,
    q_w,
    o_w,
    gate_w,
    up_w,
    down_w,
    x_all,
    s_all,
    normed,
    stream_ref,
    kv_all,
    mask_out,
    mask_all,
    scores,
    part_one,
    got_one,
    part_two,
    got_two,
    own_ref,
    w_sem,
    kv_own_sem,
    x_send,
    x_recv,
    x_pass,
    s_send,
    s_recv,
    s_pass,
    kv_send,
    kv_recv,
    kv_pass,
    m_send,
    m_recv,
    m_pass,
    one_send,
    one_recv,
    two_send,
    two_recv,
):
    devices, rows, cols = x_all.shape
    chips = devices // 2
    group = cols // HEAD_DIM
    me = lax.axis_index("seq")
    chip = me // 2
    core = me % 2
    partner = chip * 2 + 1 - core

    def fetch(k, src, dst):
        return pltpu.make_async_copy(src, dst, w_sem.at[k])

    def remote(src, dst, send, recv, device):
        return pltpu.make_async_remote_copy(
            src_ref=src,
            dst_ref=dst,
            send_sem=send,
            recv_sem=recv,
            device_id={"seq": device},
            device_id_type=pl.DeviceIdType.MESH,
        )

    def chip_at(off):
        return (chip + off) % chips

    def gather_start(src, dst, send, recv):
        for off in FAR_FIRST:
            remote(src, dst.at[me], send.at[off], recv.at[me], chip_at(off) * 2 + core).start()
        remote(src, dst.at[me], send.at[0], recv.at[me], partner).start()

    def gather_pass(dst, send, recv, hand):
        for off in reversed(FAR_FIRST):
            other = chip_at(off) * 2 + core
            remote(dst.at[other], dst.at[other], send.at[off], recv.at[other], partner).wait_recv()
            remote(dst.at[other], dst.at[other], hand.at[off], recv.at[other], partner).start()

    def gather_finish(dst, send, recv):
        for off in range(chips):
            other = chip_at(off) * 2 + 1 - core
            remote(dst.at[other], dst.at[other], send.at[0], recv.at[other], partner).wait_recv()

    def gather_drain(src, dst, send, recv, hand):
        for off in range(chips):
            remote(src, dst.at[me], send.at[off], recv.at[me], partner).wait_send()
        for off in FAR_FIRST:
            remote(src, dst.at[me], hand.at[off], recv.at[me], partner).wait_send()

    fetch_q = fetch(0, q_hbm, q_w)
    fetch_o = fetch(1, o_hbm, o_w)
    fetch_gate = fetch(2, gate_hbm, gate_w)
    fetch_up = fetch(3, up_hbm, up_w)
    fetch_down = fetch(4, down_hbm, down_w)

    barrier = pltpu.get_barrier_semaphore()
    for off in range(1, devices):
        pl.semaphore_signal(
            barrier,
            inc=1,
            device_id={"seq": (me + off) % devices},
            device_id_type=pl.DeviceIdType.MESH,
        )
    fetch_q.start()
    own_kv = pltpu.make_async_copy(
        kv_hbm.at[:, :, pl.ds(pl.multiple_of(chip * HEAD_DIM, HEAD_DIM), HEAD_DIM)],
        kv_all.at[me],
        kv_own_sem,
    )
    own_kv.start()
    fetch_o.start()
    for g in range(KV_HEADS):
        mask_out[g] = jnp.broadcast_to(
            mask_ref[:, g : g + 1].astype(jnp.float32), (rows, HEAD_DIM)
        )
    mask_all[me] = mask_out[chip]
    x_all[me] = x_ref[...]
    pl.semaphore_wait(barrier, devices - 1)

    gather_start(x_ref, x_all, x_send, x_recv)

    def kv_of(where):
        return kv_hbm.at[:, :, pl.ds(pl.multiple_of(where * HEAD_DIM, HEAD_DIM), HEAD_DIM)]

    for off in FAR_FIRST:
        there = chip_at(off)
        to = there * 2 + core
        remote(kv_of(there), kv_all.at[me], kv_send.at[off], kv_recv.at[me], to).start()
        remote(mask_out.at[there], mask_all.at[me], m_send.at[off], m_recv.at[me], to).start()
    remote(kv_of(chip), kv_all.at[me], kv_send.at[0], kv_recv.at[me], partner).start()
    remote(mask_out.at[chip], mask_all.at[me], m_send.at[0], m_recv.at[me], partner).start()
    fetch_gate.start()
    fetch_up.start()
    fetch_down.start()

    def norm(values, gain):
        squares = jnp.zeros((rows, cols), jnp.float32)
        for i in range(devices):
            wide = values[i].astype(jnp.float32)
            squares = squares + wide * wide
        mean = jnp.sum(squares, axis=-1, keepdims=True) * (1.0 / (devices * cols))
        inverse = lax.rsqrt(mean + eps)
        for i in range(devices):
            part_gain = gain[i * cols : (i + 1) * cols].astype(jnp.float32).reshape(1, cols)
            normed[i] = (values[i].astype(jnp.float32) * inverse * part_gain).astype(jnp.bfloat16)

    gather_pass(x_all, x_send, x_recv, x_pass)
    gather_finish(x_all, x_send, x_recv)
    norm(x_all, attn_gain)
    fetch_q.wait()
    step = 4

    def q_step(t, total):
        for u in range(step):
            i = t * step + u
            total = total + jnp.dot(
                normed[i],
                q_w[pl.ds(pl.multiple_of(i * cols, cols), cols), :],
                preferred_element_type=jnp.float32,
            )
        return total

    queries = lax.fori_loop(
        0, devices // step, q_step, jnp.zeros((rows, cols), jnp.float32)
    ).astype(jnp.bfloat16)
    query = jnp.concatenate(
        [queries[:, h * HEAD_DIM : (h + 1) * HEAD_DIM] for h in range(group)], axis=0
    )

    gather_pass(kv_all, kv_send, kv_recv, kv_pass)
    gather_pass(mask_all, m_send, m_recv, m_pass)
    own_kv.wait()
    gather_finish(kv_all, kv_send, kv_recv)
    gather_finish(mask_all, m_send, m_recv)

    def live_at(c):
        return jnp.concatenate([mask_all[c]] * group, axis=0) > 0.5

    tops = []
    for c in range(devices):
        score = (
            lax.dot_general(
                query,
                kv_all[c, 0],
                (((1,), (1,)), ((), ())),
                preferred_element_type=jnp.float32,
            )
            * SCALE
        )
        masked = jnp.where(live_at(c), score, floor_score)
        scores[c] = masked
        tops.append(jnp.max(masked, axis=-1, keepdims=True))
    top = functools.reduce(jnp.maximum, tops)
    total = jnp.zeros((group * rows, 1), jnp.float32)
    accum = jnp.zeros((group * rows, HEAD_DIM), jnp.float32)
    for c in range(devices):
        weight = jnp.where(live_at(c), jnp.exp(scores[c] - tops[c]), 0.0)
        factor = jnp.exp(tops[c] - top)
        total = total + factor * jnp.sum(weight, axis=-1, keepdims=True)
        accum = accum + factor * jnp.dot(
            weight.astype(jnp.bfloat16), kv_all[c, 1], preferred_element_type=jnp.float32
        )
    ratio = accum / total
    attended = jnp.concatenate(
        [ratio[h * rows : (h + 1) * rows] for h in range(group)], axis=1
    ).astype(jnp.bfloat16)

    def scatter(values, weight, part, got, send, recv):
        def target(s):
            off = devices // 2 + ((s + 1) // 2) * (1 - 2 * (s % 2))
            return (me + off) % devices

        def post(s):
            to = target(s)
            remote(part.at[to], got.at[me], send.at[s], recv.at[me], to).start()

        def product(s):
            to = target(s)
            return jnp.dot(
                values,
                weight[:, pl.ds(pl.multiple_of(to * cols, cols), cols)],
                preferred_element_type=jnp.float32,
            )

        def turn(t, _):
            first = product(2 * t)
            second = product(2 * t + 1)
            part[target(2 * t)] = first.astype(part.dtype)
            part[target(2 * t + 1)] = second.astype(part.dtype)
            own_ref[...] = second

            @pl.when(t > 0)
            def _():
                post(2 * t - 2)
                post(2 * t - 1)

            return 0

        lax.fori_loop(0, devices // 2, turn, 0)
        post(devices - 2)

        def add(s, total):
            other = target(devices - 2 - s)
            remote(part.at[other], got.at[other], send.at[s], recv.at[other], other).wait_recv()
            return total + got[other].astype(jnp.float32)

        return lax.fori_loop(0, devices - 1, add, own_ref[...])

    def scatter_drain(part, got, send, recv):
        for s in range(devices - 1):
            remote(part.at[0], got.at[me], send.at[s], recv.at[me], partner).wait_send()

    fetch_o.wait()
    attn_out = scatter(attended, o_w, part_one, got_one, one_send, one_recv)
    stream = (x_ref[...].astype(jnp.float32) + attn_out).astype(jnp.bfloat16)
    stream_ref[...] = stream
    s_all[me] = stream
    gather_start(stream_ref, s_all, s_send, s_recv)
    gather_pass(s_all, s_send, s_recv, s_pass)
    gather_finish(s_all, s_send, s_recv)
    norm(s_all, mlp_gain)
    fetch_gate.wait()
    fetch_up.wait()
    wide = gate_w.shape[1]

    def ff_step(t, sums):
        gate, upward = sums
        for u in range(2):
            i = t * 2 + u
            at = pl.ds(pl.multiple_of(i * cols, cols), cols)
            gate = gate + jnp.dot(normed[i], gate_w[at, :], preferred_element_type=jnp.float32)
            upward = upward + jnp.dot(normed[i], up_w[at, :], preferred_element_type=jnp.float32)
        return gate, upward

    zeros = jnp.zeros((rows, wide), jnp.float32)
    gate, upward = lax.fori_loop(0, devices // 2, ff_step, (zeros, zeros))
    hidden = (gate / (1.0 + jnp.exp(-gate)) * upward).astype(jnp.bfloat16)
    fetch_down.wait()
    down_out = scatter(hidden, down_w, part_two, got_two, two_send, two_recv)
    y_ref[...] = (stream_ref[...].astype(jnp.float32) + down_out).astype(jnp.bfloat16)

    gather_drain(x_ref, x_all, x_send, x_recv, x_pass)
    gather_drain(kv_of(chip), kv_all, kv_send, kv_recv, kv_pass)
    gather_drain(mask_out.at[0], mask_all, m_send, m_recv, m_pass)
    gather_drain(stream_ref, s_all, s_send, s_recv, s_pass)
    scatter_drain(part_one, got_one, one_send, one_recv)
    scatter_drain(part_two, got_two, two_send, two_recv)


def layer(
    x_rows,
    attn_gain,
    q_weight,
    o_weight,
    mlp_gain,
    gate_weight,
    up_weight,
    down_weight,
    kv_cache,
    block_mask,
):
    rows, cols = x_rows.shape
    devices = lax.axis_size("seq")
    chips = devices // 2
    wide = gate_weight.shape[1]
    dma = pltpu.SemaphoreType.DMA
    held = pl.BlockSpec(memory_space=pltpu.VMEM)
    left = pl.BlockSpec(memory_space=pl.ANY)
    exchange = pltpu.VMEM((devices, rows, cols), jnp.bfloat16)
    return pl.pallas_call(
        layer_kernel,
        name="layer",
        out_shape=jax.ShapeDtypeStruct((rows, cols), jnp.bfloat16),
        in_specs=[held, held, left, left, held, left, left, left, left, held],
        out_specs=held,
        scratch_shapes=[
            pltpu.VMEM(q_weight.shape, jnp.bfloat16),
            pltpu.VMEM(o_weight.shape, jnp.bfloat16),
            pltpu.VMEM(gate_weight.shape, jnp.bfloat16),
            pltpu.VMEM(up_weight.shape, jnp.bfloat16),
            pltpu.VMEM(down_weight.shape, jnp.bfloat16),
            exchange,
            exchange,
            exchange,
            pltpu.VMEM((rows, cols), jnp.bfloat16),
            pltpu.VMEM((devices, 2, BLOCK, HEAD_DIM), jnp.bfloat16),
            pltpu.VMEM((KV_HEADS, rows, HEAD_DIM), jnp.float32),
            pltpu.VMEM((devices, rows, HEAD_DIM), jnp.float32),
            pltpu.VMEM((devices, rows * cols // HEAD_DIM, BLOCK), jnp.float32),
            exchange,
            exchange,
            exchange,
            exchange,
            pltpu.VMEM((rows, cols), jnp.float32),
            dma((5,)),
            dma(()),
            *([dma((chips,)), dma((devices,)), dma((chips,))] * 4),
            *([dma((devices,))] * 4),
        ],
        compiler_params=pltpu.CompilerParams(
            collective_id=0, has_side_effects=True, vmem_limit_bytes=67043328
        ),
    )(
        x_rows,
        attn_gain,
        q_weight,
        o_weight,
        mlp_gain,
        gate_weight,
        up_weight,
        down_weight,
        kv_cache,
        block_mask[:, :, 0],
    )


def solution(mesh):
    fused = mesh.shape["seq"] == 2 * KV_HEADS
    return jax.shard_map(
        layer if fused else local,
        mesh=mesh,
        in_specs=(
            P("group", "seq"),
            P(),
            P(None, "seq"),
            P("seq", None),
            P(),
            P(None, "seq"),
            P(None, "seq"),
            P("seq", None),
            P(None, ("group", "seq"), None),
            P("group", None, "seq"),
        ),
        out_specs=P("group", "seq"),
        check_vma=False,
    )
```

```python
import functools

import jax
import jax.numpy as jnp
from jax import lax
from jax.experimental import pallas as pl
from jax.experimental.pallas import tpu as pltpu
from jax.sharding import PartitionSpec as P

HEADS = 64
KV_HEADS = 8
HEAD_DIM = 128
BLOCK = 128


eps = 1e-05
floor_score = -1e30


def combined_all(x, axis, combine):
    everything = jax.tree.map(lambda part: lax.all_gather(part, axis), x)
    initial = jax.tree.map(lambda part: part[0], everything)

    def turn(k, so_far):
        return combine(so_far, jax.tree.map(lambda part: part[k], everything))

    return lax.fori_loop(1, lax.axis_size(axis), turn, initial)


def rms_norm(values, gain):
    wide = values.astype(jnp.float32)
    inverse = lax.rsqrt(jnp.mean(wide * wide, axis=-1, keepdims=True) + eps)
    return (wide * inverse * gain.astype(jnp.float32)).astype(jnp.bfloat16)


def combine_states(first, second):
    top_a, total_a, accum_a = first
    top_b, total_b, accum_b = second
    top = jnp.maximum(top_a, top_b)
    factor_a = jnp.exp(top_a - top)
    factor_b = jnp.exp(top_b - top)
    return (
        top,
        total_a * factor_a + total_b * factor_b,
        accum_a * factor_a[..., None] + accum_b * factor_b[..., None],
    )


def local(
    x_rows,
    attn_gain,
    q_weight,
    o_weight,
    mlp_gain,
    gate_weight,
    up_weight,
    down_weight,
    kv_cache,
    block_mask,
):
    rows = x_rows.shape[0]
    group = HEADS // KV_HEADS
    key_len = kv_cache.shape[1]
    spans = key_len // BLOCK
    scale = 1.0 / HEAD_DIM**0.5
    whole = lax.all_gather(x_rows, "seq", axis=1, tiled=True)
    normed = rms_norm(whole, attn_gain)
    query_part = jnp.dot(normed, q_weight, preferred_element_type=jnp.float32).astype(jnp.bfloat16)
    queries = lax.all_gather(query_part, "seq", axis=1, tiled=True)
    doc_keys = kv_cache[0]
    doc_values = kv_cache[1]

    def one_group(index):
        query_group = lax.dynamic_slice_in_dim(
            queries, index * (group * HEAD_DIM), group * HEAD_DIM, 1
        ).reshape(rows, group, HEAD_DIM)
        key_group = lax.dynamic_slice_in_dim(doc_keys, index * HEAD_DIM, HEAD_DIM, 1)
        value_group = lax.dynamic_slice_in_dim(doc_values, index * HEAD_DIM, HEAD_DIM, 1)
        mask_group = lax.dynamic_slice_in_dim(block_mask, index, 1, 1)[:, 0, :]
        scores = (
            jnp.einsum("rhd,kd->rhk", query_group, key_group, preferred_element_type=jnp.float32)
            * scale
        )
        scores = scores.reshape(rows, group, spans, BLOCK)
        live = (mask_group == 1)[:, None, :, None]
        masked = jnp.where(live, scores, floor_score)
        local_top = jnp.max(masked, axis=(2, 3))
        weights = jnp.where(live, jnp.exp(masked - local_top[..., None, None]), 0.0)
        local_total = jnp.sum(weights, axis=(2, 3))
        rounded = weights.astype(jnp.bfloat16).reshape(rows, group, key_len)
        local_accum = jnp.einsum(
            "rhk,kd->rhd", rounded, value_group, preferred_element_type=jnp.float32
        )
        return (local_top, local_total, local_accum)

    tops, totals, accums = lax.map(one_group, jnp.arange(KV_HEADS, dtype=jnp.int32))
    local_top = jnp.moveaxis(tops, 0, 1)
    local_total = jnp.moveaxis(totals, 0, 1)
    local_accum = jnp.moveaxis(accums, 0, 1)
    columns = q_weight.shape[1]
    col_start = lax.axis_index("seq") * columns
    top, total, accum = combined_all((local_top, local_total, local_accum), "seq", combine_states)
    attended = accum / total[..., None]
    attended = attended.reshape(rows, HEADS * HEAD_DIM).astype(jnp.bfloat16)
    attn_cols = lax.dynamic_slice_in_dim(attended, col_start, columns, 1)
    weight_cols = o_weight
    attn_out = lax.psum_scatter(
        lax.dot_general(
            weight_cols, attn_cols, (((0,), (1,)), ((), ())), preferred_element_type=jnp.float32
        ),
        "seq",
        scatter_dimension=0,
        tiled=True,
    )
    stream = (x_rows.astype(jnp.float32) + attn_out.T).astype(jnp.bfloat16)
    stream_whole = lax.all_gather(stream, "seq", axis=1, tiled=True)
    normed_two = rms_norm(stream_whole, mlp_gain)
    gate = jnp.dot(normed_two, gate_weight, preferred_element_type=jnp.float32)
    upward = jnp.dot(normed_two, up_weight, preferred_element_type=jnp.float32)
    hidden = (jax.nn.silu(gate) * upward).astype(jnp.bfloat16)
    weight_cols = down_weight
    down_out = lax.psum_scatter(
        lax.dot_general(
            weight_cols, hidden, (((0,), (1,)), ((), ())), preferred_element_type=jnp.float32
        ),
        "seq",
        scatter_dimension=0,
        tiled=True,
    )
    return (stream.astype(jnp.float32) + down_out.T).astype(jnp.bfloat16)


FAR_FIRST = (4, 3, 5, 2, 6, 1, 7)
SCALE = 1.0 / HEAD_DIM**0.5


def layer_kernel(
    x_ref,
    attn_gain,
    q_hbm,
    o_hbm,
    mlp_gain,
    gate_hbm,
    up_hbm,
    down_hbm,
    kv_hbm,
    mask_ref,
    y_ref,
    q_w,
    o_w,
    gate_w,
    up_w,
    down_w,
    x_all,
    s_all,
    normed,
    stream_ref,
    kv_all,
    mask_out,
    mask_all,
    scores,
    pair_out,
    pair_in,
    part_one,
    got_one,
    part_two,
    got_two,
    own_ref,
    w_sem,
    kv_own_sem,
    x_send,
    x_recv,
    x_pass,
    s_send,
    s_recv,
    s_pass,
    kv_send,
    kv_recv,
    kv_pass,
    m_send,
    m_recv,
    m_pass,
    *scatter_sems,
):
    one_sems, two_sems = scatter_sems[:4], scatter_sems[4:]
    devices, rows, cols = x_all.shape
    chips = devices // 2
    group = cols // HEAD_DIM
    me = lax.axis_index("seq")
    chip = me // 2
    core = me % 2
    partner = chip * 2 + 1 - core

    def fetch(k, src, dst):
        return pltpu.make_async_copy(src, dst, w_sem.at[k])

    def remote(src, dst, send, recv, device):
        return pltpu.make_async_remote_copy(
            src_ref=src,
            dst_ref=dst,
            send_sem=send,
            recv_sem=recv,
            device_id={"seq": device},
            device_id_type=pl.DeviceIdType.MESH,
        )

    def chip_at(off):
        return (chip + off) % chips

    def gather_start(src, dst, send, recv):
        for off in FAR_FIRST:
            remote(src, dst.at[me], send.at[off], recv.at[me], chip_at(off) * 2 + core).start()
        remote(src, dst.at[me], send.at[0], recv.at[me], partner).start()

    def gather_pass(dst, send, recv, hand):
        for off in reversed(FAR_FIRST):
            other = chip_at(off) * 2 + core
            remote(dst.at[other], dst.at[other], send.at[off], recv.at[other], partner).wait_recv()
            remote(dst.at[other], dst.at[other], hand.at[off], recv.at[other], partner).start()

    def gather_finish(dst, send, recv):
        for off in range(chips):
            other = chip_at(off) * 2 + 1 - core
            remote(dst.at[other], dst.at[other], send.at[0], recv.at[other], partner).wait_recv()

    def gather_drain(src, dst, send, recv, hand):
        for off in range(chips):
            remote(src, dst.at[me], send.at[off], recv.at[me], partner).wait_send()
        for off in FAR_FIRST:
            remote(src, dst.at[me], hand.at[off], recv.at[me], partner).wait_send()

    fetch_q = fetch(0, q_hbm, q_w)
    fetch_o = fetch(1, o_hbm, o_w)
    fetch_gate = fetch(2, gate_hbm, gate_w)
    fetch_up = fetch(3, up_hbm, up_w)
    fetch_down = fetch(4, down_hbm, down_w)

    barrier = pltpu.get_barrier_semaphore()
    for off in range(1, devices):
        pl.semaphore_signal(
            barrier,
            inc=1,
            device_id={"seq": (me + off) % devices},
            device_id_type=pl.DeviceIdType.MESH,
        )
    fetch_q.start()
    own_kv = pltpu.make_async_copy(
        kv_hbm.at[:, :, pl.ds(pl.multiple_of(chip * HEAD_DIM, HEAD_DIM), HEAD_DIM)],
        kv_all.at[me],
        kv_own_sem,
    )
    own_kv.start()
    fetch_o.start()
    for g in range(KV_HEADS):
        mask_out[g] = jnp.broadcast_to(
            mask_ref[:, g : g + 1].astype(jnp.float32), (rows, HEAD_DIM)
        )
    mask_all[me] = mask_out[chip]
    x_all[me] = x_ref[...]
    pl.semaphore_wait(barrier, devices - 1)

    gather_start(x_ref, x_all, x_send, x_recv)

    def kv_of(where):
        return kv_hbm.at[:, :, pl.ds(pl.multiple_of(where * HEAD_DIM, HEAD_DIM), HEAD_DIM)]

    for off in FAR_FIRST:
        there = chip_at(off)
        to = there * 2 + core
        remote(kv_of(there), kv_all.at[me], kv_send.at[off], kv_recv.at[me], to).start()
        remote(mask_out.at[there], mask_all.at[me], m_send.at[off], m_recv.at[me], to).start()
    remote(kv_of(chip), kv_all.at[me], kv_send.at[0], kv_recv.at[me], partner).start()
    remote(mask_out.at[chip], mask_all.at[me], m_send.at[0], m_recv.at[me], partner).start()
    fetch_gate.start()
    fetch_up.start()
    fetch_down.start()

    def norm(values, gain):
        squares = jnp.zeros((rows, cols), jnp.float32)
        for i in range(devices):
            wide = values[i].astype(jnp.float32)
            squares = squares + wide * wide
        mean = jnp.sum(squares, axis=-1, keepdims=True) * (1.0 / (devices * cols))
        inverse = lax.rsqrt(mean + eps)
        for i in range(devices):
            part_gain = gain[i * cols : (i + 1) * cols].astype(jnp.float32).reshape(1, cols)
            normed[i] = (values[i].astype(jnp.float32) * inverse * part_gain).astype(jnp.bfloat16)

    gather_pass(x_all, x_send, x_recv, x_pass)
    gather_finish(x_all, x_send, x_recv)
    norm(x_all, attn_gain)
    fetch_q.wait()
    step = 4

    def q_step(t, total):
        for u in range(step):
            i = t * step + u
            total = total + jnp.dot(
                normed[i],
                q_w[pl.ds(pl.multiple_of(i * cols, cols), cols), :],
                preferred_element_type=jnp.float32,
            )
        return total

    queries = lax.fori_loop(
        0, devices // step, q_step, jnp.zeros((rows, cols), jnp.float32)
    ).astype(jnp.bfloat16)
    query = jnp.concatenate(
        [queries[:, h * HEAD_DIM : (h + 1) * HEAD_DIM] for h in range(group)], axis=0
    )

    gather_pass(kv_all, kv_send, kv_recv, kv_pass)
    gather_pass(mask_all, m_send, m_recv, m_pass)
    own_kv.wait()
    gather_finish(kv_all, kv_send, kv_recv)
    gather_finish(mask_all, m_send, m_recv)

    def live_at(c):
        return jnp.concatenate([mask_all[c]] * group, axis=0) > 0.5

    tops = []
    for c in range(devices):
        score = (
            lax.dot_general(
                query,
                kv_all[c, 0],
                (((1,), (1,)), ((), ())),
                preferred_element_type=jnp.float32,
            )
            * SCALE
        )
        masked = jnp.where(live_at(c), score, floor_score)
        scores[c] = masked
        tops.append(jnp.max(masked, axis=-1, keepdims=True))
    top = functools.reduce(jnp.maximum, tops)
    total = jnp.zeros((group * rows, 1), jnp.float32)
    accum = jnp.zeros((group * rows, HEAD_DIM), jnp.float32)
    for c in range(devices):
        weight = jnp.where(live_at(c), jnp.exp(scores[c] - tops[c]), 0.0)
        factor = jnp.exp(tops[c] - top)
        total = total + factor * jnp.sum(weight, axis=-1, keepdims=True)
        accum = accum + factor * jnp.dot(
            weight.astype(jnp.bfloat16), kv_all[c, 1], preferred_element_type=jnp.float32
        )
    ratio = accum / total
    attended = jnp.concatenate(
        [ratio[h * rows : (h + 1) * rows] for h in range(group)], axis=1
    ).astype(jnp.bfloat16)

    def scatter(values, weight, pair_out, pair_in, part, got, sems):
        pair_send, pair_recv, send, recv = sems

        def chip_of(s):
            off = chips // 2 + ((s + 1) // 2) * (1 - 2 * (s % 2))
            return chip_at(off)

        def product(where, half):
            to = where * 2 + half
            return jnp.dot(
                values,
                weight[:, pl.ds(pl.multiple_of(to * cols, cols), cols)],
                preferred_element_type=jnp.float32,
            )

        def to_partner(s):
            to = chip_of(s)
            return remote(pair_out.at[to], pair_in.at[to], pair_send.at[s], pair_recv.at[to], partner)

        def to_chip(s):
            to = chip_of(s)
            return remote(part.at[to], got.at[chip], send.at[s], recv.at[chip], to * 2 + core)

        def pair_turn(t, _):
            first = product(chip_of(2 * t), 1 - core)
            second = product(chip_of(2 * t + 1), 1 - core)
            pair_out[chip_of(2 * t)] = first
            pair_out[chip_of(2 * t + 1)] = second

            @pl.when(t > 0)
            def _():
                to_partner(2 * t - 2).start()
                to_partner(2 * t - 1).start()

            return 0

        lax.fori_loop(0, chips // 2, pair_turn, 0)

        def chip_turn(t, _):
            one, two = chip_of(2 * t), chip_of(2 * t + 1)
            first = product(one, core)
            second = product(two, core)

            @pl.when(t == 0)
            def _():
                to_partner(chips - 2).start()
                to_partner(chips - 1).start()

            to_partner(2 * t).wait_recv()
            to_partner(2 * t + 1).wait_recv()
            second = second + pair_in[two]
            part[one] = (first + pair_in[one]).astype(part.dtype)
            part[two] = second.astype(part.dtype)
            own_ref[...] = second

            @pl.when(t > 0)
            def _():
                to_chip(2 * t - 2).start()
                to_chip(2 * t - 1).start()

            return 0

        lax.fori_loop(0, chips // 2, chip_turn, 0)
        to_chip(chips - 2).start()
        total = own_ref[...]
        for off in reversed(FAR_FIRST):
            other = chip_at(off)
            remote(part.at[other], got.at[other], send.at[0], recv.at[other], partner).wait_recv()
            total = total + got[other].astype(jnp.float32)
        for s in range(chips):
            to_partner(s).wait_send()
        return total

    def scatter_drain(part, got, sems):
        _, _, send, recv = sems
        for s in range(chips - 1):
            remote(part.at[0], got.at[chip], send.at[s], recv.at[chip], partner).wait_send()

    fetch_o.wait()
    attn_out = scatter(attended, o_w, pair_out, pair_in, part_one, got_one, one_sems)
    stream = (x_ref[...].astype(jnp.float32) + attn_out).astype(jnp.bfloat16)
    stream_ref[...] = stream
    s_all[me] = stream
    gather_start(stream_ref, s_all, s_send, s_recv)
    gather_pass(s_all, s_send, s_recv, s_pass)
    gather_finish(s_all, s_send, s_recv)
    norm(s_all, mlp_gain)
    fetch_gate.wait()
    fetch_up.wait()
    wide = gate_w.shape[1]

    def ff_step(t, sums):
        gate, upward = sums
        for u in range(2):
            i = t * 2 + u
            at = pl.ds(pl.multiple_of(i * cols, cols), cols)
            gate = gate + jnp.dot(normed[i], gate_w[at, :], preferred_element_type=jnp.float32)
            upward = upward + jnp.dot(normed[i], up_w[at, :], preferred_element_type=jnp.float32)
        return gate, upward

    zeros = jnp.zeros((rows, wide), jnp.float32)
    gate, upward = lax.fori_loop(0, devices // 2, ff_step, (zeros, zeros))
    hidden = (gate / (1.0 + jnp.exp(-gate)) * upward).astype(jnp.bfloat16)
    fetch_down.wait()
    down_out = scatter(hidden, down_w, pair_out, pair_in, part_two, got_two, two_sems)
    y_ref[...] = (stream_ref[...].astype(jnp.float32) + down_out).astype(jnp.bfloat16)

    gather_drain(x_ref, x_all, x_send, x_recv, x_pass)
    gather_drain(kv_of(chip), kv_all, kv_send, kv_recv, kv_pass)
    gather_drain(mask_out.at[0], mask_all, m_send, m_recv, m_pass)
    gather_drain(stream_ref, s_all, s_send, s_recv, s_pass)
    scatter_drain(part_one, got_one, one_sems)
    scatter_drain(part_two, got_two, two_sems)


def layer(
    x_rows,
    attn_gain,
    q_weight,
    o_weight,
    mlp_gain,
    gate_weight,
    up_weight,
    down_weight,
    kv_cache,
    block_mask,
):
    rows, cols = x_rows.shape
    devices = lax.axis_size("seq")
    chips = devices // 2
    wide = gate_weight.shape[1]
    dma = pltpu.SemaphoreType.DMA
    held = pl.BlockSpec(memory_space=pltpu.VMEM)
    left = pl.BlockSpec(memory_space=pl.ANY)
    half = pltpu.VMEM((chips, rows, cols), jnp.bfloat16)
    wide_half = pltpu.VMEM((chips, rows, cols), jnp.float32)
    exchange = pltpu.VMEM((devices, rows, cols), jnp.bfloat16)
    return pl.pallas_call(
        layer_kernel,
        name="layer",
        out_shape=jax.ShapeDtypeStruct((rows, cols), jnp.bfloat16),
        in_specs=[held, held, left, left, held, left, left, left, left, held],
        out_specs=held,
        scratch_shapes=[
            pltpu.VMEM(q_weight.shape, jnp.bfloat16),
            pltpu.VMEM(o_weight.shape, jnp.bfloat16),
            pltpu.VMEM(gate_weight.shape, jnp.bfloat16),
            pltpu.VMEM(up_weight.shape, jnp.bfloat16),
            pltpu.VMEM(down_weight.shape, jnp.bfloat16),
            exchange,
            exchange,
            exchange,
            pltpu.VMEM((rows, cols), jnp.bfloat16),
            pltpu.VMEM((devices, 2, BLOCK, HEAD_DIM), jnp.bfloat16),
            pltpu.VMEM((KV_HEADS, rows, HEAD_DIM), jnp.float32),
            pltpu.VMEM((devices, rows, HEAD_DIM), jnp.float32),
            pltpu.VMEM((devices, rows * cols // HEAD_DIM, BLOCK), jnp.float32),
            wide_half,
            wide_half,
            wide_half,
            wide_half,
            half,
            half,
            pltpu.VMEM((rows, cols), jnp.float32),
            dma((5,)),
            dma(()),
            *([dma((chips,)), dma((devices,)), dma((chips,))] * 4),
            *([dma((chips,))] * 8),
        ],
        compiler_params=pltpu.CompilerParams(
            collective_id=0, has_side_effects=True, vmem_limit_bytes=67043328
        ),
    )(
        x_rows,
        attn_gain,
        q_weight,
        o_weight,
        mlp_gain,
        gate_weight,
        up_weight,
        down_weight,
        kv_cache,
        block_mask[:, :, 0],
    )


def solution(mesh):
    fused = mesh.shape["seq"] == 2 * KV_HEADS
    return jax.shard_map(
        layer if fused else local,
        mesh=mesh,
        in_specs=(
            P("group", "seq"),
            P(),
            P(None, "seq"),
            P("seq", None),
            P(),
            P(None, "seq"),
            P(None, "seq"),
            P("seq", None),
            P(None, ("group", "seq"), None),
            P("group", None, "seq"),
        ),
        out_specs=P("group", "seq"),
        check_vma=False,
    )
```

```python
import functools

import jax
import jax.numpy as jnp
from jax import lax
from jax.experimental import pallas as pl
from jax.experimental.pallas import tpu as pltpu
from jax.sharding import PartitionSpec as P

HEADS = 64
KV_HEADS = 8
HEAD_DIM = 128
BLOCK = 128


eps = 1e-05
floor_score = -1e30


def combined_all(x, axis, combine):
    everything = jax.tree.map(lambda part: lax.all_gather(part, axis), x)
    initial = jax.tree.map(lambda part: part[0], everything)

    def turn(k, so_far):
        return combine(so_far, jax.tree.map(lambda part: part[k], everything))

    return lax.fori_loop(1, lax.axis_size(axis), turn, initial)


def rms_norm(values, gain):
    wide = values.astype(jnp.float32)
    inverse = lax.rsqrt(jnp.mean(wide * wide, axis=-1, keepdims=True) + eps)
    return (wide * inverse * gain.astype(jnp.float32)).astype(jnp.bfloat16)


def combine_states(first, second):
    top_a, total_a, accum_a = first
    top_b, total_b, accum_b = second
    top = jnp.maximum(top_a, top_b)
    factor_a = jnp.exp(top_a - top)
    factor_b = jnp.exp(top_b - top)
    return (
        top,
        total_a * factor_a + total_b * factor_b,
        accum_a * factor_a[..., None] + accum_b * factor_b[..., None],
    )


def local(
    x_rows,
    attn_gain,
    q_weight,
    o_weight,
    mlp_gain,
    gate_weight,
    up_weight,
    down_weight,
    kv_cache,
    block_mask,
):
    rows = x_rows.shape[0]
    group = HEADS // KV_HEADS
    key_len = kv_cache.shape[1]
    spans = key_len // BLOCK
    scale = 1.0 / HEAD_DIM**0.5
    whole = lax.all_gather(x_rows, "seq", axis=1, tiled=True)
    normed = rms_norm(whole, attn_gain)
    query_part = jnp.dot(normed, q_weight, preferred_element_type=jnp.float32).astype(jnp.bfloat16)
    queries = lax.all_gather(query_part, "seq", axis=1, tiled=True)
    doc_keys = kv_cache[0]
    doc_values = kv_cache[1]

    def one_group(index):
        query_group = lax.dynamic_slice_in_dim(
            queries, index * (group * HEAD_DIM), group * HEAD_DIM, 1
        ).reshape(rows, group, HEAD_DIM)
        key_group = lax.dynamic_slice_in_dim(doc_keys, index * HEAD_DIM, HEAD_DIM, 1)
        value_group = lax.dynamic_slice_in_dim(doc_values, index * HEAD_DIM, HEAD_DIM, 1)
        mask_group = lax.dynamic_slice_in_dim(block_mask, index, 1, 1)[:, 0, :]
        scores = (
            jnp.einsum("rhd,kd->rhk", query_group, key_group, preferred_element_type=jnp.float32)
            * scale
        )
        scores = scores.reshape(rows, group, spans, BLOCK)
        live = (mask_group == 1)[:, None, :, None]
        masked = jnp.where(live, scores, floor_score)
        local_top = jnp.max(masked, axis=(2, 3))
        weights = jnp.where(live, jnp.exp(masked - local_top[..., None, None]), 0.0)
        local_total = jnp.sum(weights, axis=(2, 3))
        rounded = weights.astype(jnp.bfloat16).reshape(rows, group, key_len)
        local_accum = jnp.einsum(
            "rhk,kd->rhd", rounded, value_group, preferred_element_type=jnp.float32
        )
        return (local_top, local_total, local_accum)

    tops, totals, accums = lax.map(one_group, jnp.arange(KV_HEADS, dtype=jnp.int32))
    local_top = jnp.moveaxis(tops, 0, 1)
    local_total = jnp.moveaxis(totals, 0, 1)
    local_accum = jnp.moveaxis(accums, 0, 1)
    columns = q_weight.shape[1]
    col_start = lax.axis_index("seq") * columns
    top, total, accum = combined_all((local_top, local_total, local_accum), "seq", combine_states)
    attended = accum / total[..., None]
    attended = attended.reshape(rows, HEADS * HEAD_DIM).astype(jnp.bfloat16)
    attn_cols = lax.dynamic_slice_in_dim(attended, col_start, columns, 1)
    weight_cols = o_weight
    attn_out = lax.psum_scatter(
        lax.dot_general(
            weight_cols, attn_cols, (((0,), (1,)), ((), ())), preferred_element_type=jnp.float32
        ),
        "seq",
        scatter_dimension=0,
        tiled=True,
    )
    stream = (x_rows.astype(jnp.float32) + attn_out.T).astype(jnp.bfloat16)
    stream_whole = lax.all_gather(stream, "seq", axis=1, tiled=True)
    normed_two = rms_norm(stream_whole, mlp_gain)
    gate = jnp.dot(normed_two, gate_weight, preferred_element_type=jnp.float32)
    upward = jnp.dot(normed_two, up_weight, preferred_element_type=jnp.float32)
    hidden = (jax.nn.silu(gate) * upward).astype(jnp.bfloat16)
    weight_cols = down_weight
    down_out = lax.psum_scatter(
        lax.dot_general(
            weight_cols, hidden, (((0,), (1,)), ((), ())), preferred_element_type=jnp.float32
        ),
        "seq",
        scatter_dimension=0,
        tiled=True,
    )
    return (stream.astype(jnp.float32) + down_out.T).astype(jnp.bfloat16)


FAR_FIRST = (4, 3, 5, 2, 6, 1, 7)
SCALE = 1.0 / HEAD_DIM**0.5


def layer_kernel(
    x_ref,
    attn_gain,
    q_hbm,
    o_hbm,
    mlp_gain,
    gate_hbm,
    up_hbm,
    down_hbm,
    kv_hbm,
    mask_ref,
    y_ref,
    q_w,
    o_w,
    gate_w,
    up_w,
    down_w,
    x_all,
    s_all,
    normed,
    stream_ref,
    kv_all,
    mask_out,
    mask_all,
    scores,
    pair_out,
    pair_in,
    part_one,
    got_one,
    part_two,
    got_two,
    own_ref,
    w_sem,
    kv_own_sem,
    x_send,
    x_recv,
    x_pass,
    s_send,
    s_recv,
    s_pass,
    kv_send,
    kv_recv,
    kv_pass,
    m_send,
    m_recv,
    m_pass,
    *scatter_sems,
):
    one_sems, two_sems = scatter_sems[:4], scatter_sems[4:]
    devices, rows, cols = x_all.shape
    chips = devices // 2
    group = cols // HEAD_DIM
    me = lax.axis_index("seq")
    chip = me // 2
    core = me % 2
    partner = chip * 2 + 1 - core

    def fetch(k, src, dst):
        return pltpu.make_async_copy(src, dst, w_sem.at[k])

    def remote(src, dst, send, recv, device):
        return pltpu.make_async_remote_copy(
            src_ref=src,
            dst_ref=dst,
            send_sem=send,
            recv_sem=recv,
            device_id={"seq": device},
            device_id_type=pl.DeviceIdType.MESH,
        )

    def chip_at(off):
        return (chip + off) % chips

    def gather_start(src, dst, send, recv):
        for off in FAR_FIRST:
            remote(src, dst.at[me], send.at[off], recv.at[me], chip_at(off) * 2 + core).start()
        remote(src, dst.at[me], send.at[0], recv.at[me], partner).start()

    def gather_pass(dst, send, recv, hand):
        for off in reversed(FAR_FIRST):
            other = chip_at(off) * 2 + core
            remote(dst.at[other], dst.at[other], send.at[off], recv.at[other], partner).wait_recv()
            remote(dst.at[other], dst.at[other], hand.at[off], recv.at[other], partner).start()

    def gather_finish(dst, send, recv):
        for off in range(chips):
            other = chip_at(off) * 2 + 1 - core
            remote(dst.at[other], dst.at[other], send.at[0], recv.at[other], partner).wait_recv()

    def gather_drain(src, dst, send, recv, hand):
        for off in range(chips):
            remote(src, dst.at[me], send.at[off], recv.at[me], partner).wait_send()
        for off in FAR_FIRST:
            remote(src, dst.at[me], hand.at[off], recv.at[me], partner).wait_send()

    fetch_q = fetch(0, q_hbm, q_w)
    fetch_o = fetch(1, o_hbm, o_w)
    fetch_gate = fetch(2, gate_hbm, gate_w)
    fetch_up = fetch(3, up_hbm, up_w)
    fetch_down = fetch(4, down_hbm, down_w)

    barrier = pltpu.get_barrier_semaphore()
    for off in range(1, devices):
        pl.semaphore_signal(
            barrier,
            inc=1,
            device_id={"seq": (me + off) % devices},
            device_id_type=pl.DeviceIdType.MESH,
        )
    span = kv_hbm.shape[1]
    stage = [
        pltpu.make_async_copy(
            kv_hbm.at[k],
            down_w.at[k * span : (k + 1) * span, : KV_HEADS * HEAD_DIM],
            kv_own_sem.at[k],
        )
        for k in range(2)
    ]
    for copy in stage:
        copy.start()
    fetch_q.start()
    for g in range(KV_HEADS):
        mask_out[g] = jnp.broadcast_to(
            mask_ref[:, g : g + 1].astype(jnp.float32), (rows, HEAD_DIM)
        )
    mask_all[me] = mask_out[chip]
    x_all[me] = x_ref[...]
    pl.semaphore_wait(barrier, devices - 1)

    gather_start(x_ref, x_all, x_send, x_recv)

    def kv_of(where):
        at = pl.ds(pl.multiple_of(where * HEAD_DIM, HEAD_DIM), HEAD_DIM)
        return down_w.at[: 2 * span, at]

    for copy in stage:
        copy.wait()
    own_kv = pltpu.make_async_copy(kv_of(chip), kv_all.at[me], kv_own_sem.at[2])
    own_kv.start()

    for off in FAR_FIRST:
        there = chip_at(off)
        to = there * 2 + core
        remote(kv_of(there), kv_all.at[me], kv_send.at[off], kv_recv.at[me], to).start()
        remote(mask_out.at[there], mask_all.at[me], m_send.at[off], m_recv.at[me], to).start()
    remote(kv_of(chip), kv_all.at[me], kv_send.at[0], kv_recv.at[me], partner).start()
    remote(mask_out.at[chip], mask_all.at[me], m_send.at[0], m_recv.at[me], partner).start()

    def norm(values, gain):
        squares = jnp.zeros((rows, cols), jnp.float32)
        for i in range(devices):
            wide = values[i].astype(jnp.float32)
            squares = squares + wide * wide
        mean = jnp.sum(squares, axis=-1, keepdims=True) * (1.0 / (devices * cols))
        inverse = lax.rsqrt(mean + eps)
        for i in range(devices):
            part_gain = gain[i * cols : (i + 1) * cols].astype(jnp.float32).reshape(1, cols)
            normed[i] = (values[i].astype(jnp.float32) * inverse * part_gain).astype(jnp.bfloat16)

    gather_pass(x_all, x_send, x_recv, x_pass)
    gather_finish(x_all, x_send, x_recv)
    fetch_o.start()
    norm(x_all, attn_gain)
    fetch_q.wait()
    step = 4

    def q_step(t, total):
        for u in range(step):
            i = t * step + u
            total = total + jnp.dot(
                normed[i],
                q_w[pl.ds(pl.multiple_of(i * cols, cols), cols), :],
                preferred_element_type=jnp.float32,
            )
        return total

    queries = lax.fori_loop(
        0, devices // step, q_step, jnp.zeros((rows, cols), jnp.float32)
    ).astype(jnp.bfloat16)
    query = jnp.concatenate(
        [queries[:, h * HEAD_DIM : (h + 1) * HEAD_DIM] for h in range(group)], axis=0
    )

    gather_pass(kv_all, kv_send, kv_recv, kv_pass)
    gather_pass(mask_all, m_send, m_recv, m_pass)
    fetch_gate.start()
    fetch_up.start()
    own_kv.wait()
    gather_finish(kv_all, kv_send, kv_recv)
    gather_finish(mask_all, m_send, m_recv)

    def live_at(c):
        return jnp.concatenate([mask_all[c]] * group, axis=0) > 0.5

    tops = []
    for c in range(devices):
        score = (
            lax.dot_general(
                query,
                kv_all[c, :span],
                (((1,), (1,)), ((), ())),
                preferred_element_type=jnp.float32,
            )
            * SCALE
        )
        masked = jnp.where(live_at(c), score, floor_score)
        scores[c] = masked
        tops.append(jnp.max(masked, axis=-1, keepdims=True))
    top = functools.reduce(jnp.maximum, tops)
    total = jnp.zeros((group * rows, 1), jnp.float32)
    accum = jnp.zeros((group * rows, HEAD_DIM), jnp.float32)
    for c in range(devices):
        weight = jnp.where(live_at(c), jnp.exp(scores[c] - tops[c]), 0.0)
        factor = jnp.exp(tops[c] - top)
        total = total + factor * jnp.sum(weight, axis=-1, keepdims=True)
        accum = accum + factor * jnp.dot(
            weight.astype(jnp.bfloat16), kv_all[c, span:], preferred_element_type=jnp.float32
        )
    ratio = accum / total
    attended = jnp.concatenate(
        [ratio[h * rows : (h + 1) * rows] for h in range(group)], axis=1
    ).astype(jnp.bfloat16)

    def scatter(values, weight, pair_out, pair_in, part, got, sems):
        pair_send, pair_recv, send, recv = sems

        def chip_of(s):
            off = chips // 2 + ((s + 1) // 2) * (1 - 2 * (s % 2))
            return chip_at(off)

        def product(where, half):
            to = where * 2 + half
            return jnp.dot(
                values,
                weight[:, pl.ds(pl.multiple_of(to * cols, cols), cols)],
                preferred_element_type=jnp.float32,
            )

        def to_partner(s):
            to = chip_of(s)
            return remote(pair_out.at[to], pair_in.at[to], pair_send.at[s], pair_recv.at[to], partner)

        def to_chip(s):
            to = chip_of(s)
            return remote(part.at[to], got.at[chip], send.at[s], recv.at[chip], to * 2 + core)

        def pair_turn(t, _):
            first = product(chip_of(2 * t), 1 - core)
            second = product(chip_of(2 * t + 1), 1 - core)
            pair_out[chip_of(2 * t)] = first
            pair_out[chip_of(2 * t + 1)] = second

            @pl.when(t > 0)
            def _():
                to_partner(2 * t - 2).start()
                to_partner(2 * t - 1).start()

            return 0

        lax.fori_loop(0, chips // 2, pair_turn, 0)

        def chip_turn(t, _):
            one, two = chip_of(2 * t), chip_of(2 * t + 1)
            first = product(one, core)
            second = product(two, core)

            @pl.when(t == 0)
            def _():
                to_partner(chips - 2).start()
                to_partner(chips - 1).start()

            to_partner(2 * t).wait_recv()
            to_partner(2 * t + 1).wait_recv()
            second = second + pair_in[two]
            part[one] = (first + pair_in[one]).astype(part.dtype)
            part[two] = second.astype(part.dtype)
            own_ref[...] = second

            @pl.when(t > 0)
            def _():
                to_chip(2 * t - 2).start()
                to_chip(2 * t - 1).start()

            return 0

        lax.fori_loop(0, chips // 2, chip_turn, 0)
        to_chip(chips - 2).start()
        total = own_ref[...]
        for off in reversed(FAR_FIRST):
            other = chip_at(off)
            remote(part.at[other], got.at[other], send.at[0], recv.at[other], partner).wait_recv()
            total = total + got[other].astype(jnp.float32)
        for s in range(chips):
            to_partner(s).wait_send()
        return total

    def scatter_drain(part, got, sems):
        _, _, send, recv = sems
        for s in range(chips - 1):
            remote(part.at[0], got.at[chip], send.at[s], recv.at[chip], partner).wait_send()

    gather_drain(kv_of(chip), kv_all, kv_send, kv_recv, kv_pass)
    fetch_down.start()
    fetch_o.wait()
    attn_out = scatter(attended, o_w, pair_out, pair_in, part_one, got_one, one_sems)
    stream = (x_ref[...].astype(jnp.float32) + attn_out).astype(jnp.bfloat16)
    stream_ref[...] = stream
    s_all[me] = stream
    gather_start(stream_ref, s_all, s_send, s_recv)
    gather_pass(s_all, s_send, s_recv, s_pass)
    gather_finish(s_all, s_send, s_recv)
    norm(s_all, mlp_gain)
    fetch_gate.wait()
    fetch_up.wait()
    wide = gate_w.shape[1]

    def ff_step(t, sums):
        gate, upward = sums
        for u in range(2):
            i = t * 2 + u
            at = pl.ds(pl.multiple_of(i * cols, cols), cols)
            gate = gate + jnp.dot(normed[i], gate_w[at, :], preferred_element_type=jnp.float32)
            upward = upward + jnp.dot(normed[i], up_w[at, :], preferred_element_type=jnp.float32)
        return gate, upward

    zeros = jnp.zeros((rows, wide), jnp.float32)
    gate, upward = lax.fori_loop(0, devices // 2, ff_step, (zeros, zeros))
    hidden = (gate / (1.0 + jnp.exp(-gate)) * upward).astype(jnp.bfloat16)
    fetch_down.wait()
    down_out = scatter(hidden, down_w, pair_out, pair_in, part_two, got_two, two_sems)
    y_ref[...] = (stream_ref[...].astype(jnp.float32) + down_out).astype(jnp.bfloat16)

    gather_drain(x_ref, x_all, x_send, x_recv, x_pass)
    gather_drain(mask_out.at[0], mask_all, m_send, m_recv, m_pass)
    gather_drain(stream_ref, s_all, s_send, s_recv, s_pass)
    scatter_drain(part_one, got_one, one_sems)
    scatter_drain(part_two, got_two, two_sems)


def layer(
    x_rows,
    attn_gain,
    q_weight,
    o_weight,
    mlp_gain,
    gate_weight,
    up_weight,
    down_weight,
    kv_cache,
    block_mask,
):
    rows, cols = x_rows.shape
    devices = lax.axis_size("seq")
    chips = devices // 2
    wide = gate_weight.shape[1]
    dma = pltpu.SemaphoreType.DMA
    held = pl.BlockSpec(memory_space=pltpu.VMEM)
    left = pl.BlockSpec(memory_space=pl.ANY)
    half = pltpu.VMEM((chips, rows, cols), jnp.bfloat16)
    wide_half = pltpu.VMEM((chips, rows, cols), jnp.float32)
    exchange = pltpu.VMEM((devices, rows, cols), jnp.bfloat16)
    return pl.pallas_call(
        layer_kernel,
        name="layer",
        out_shape=jax.ShapeDtypeStruct((rows, cols), jnp.bfloat16),
        in_specs=[held, held, left, left, held, left, left, left, left, held],
        out_specs=held,
        scratch_shapes=[
            pltpu.VMEM(q_weight.shape, jnp.bfloat16),
            pltpu.VMEM(o_weight.shape, jnp.bfloat16),
            pltpu.VMEM(gate_weight.shape, jnp.bfloat16),
            pltpu.VMEM(up_weight.shape, jnp.bfloat16),
            pltpu.VMEM(down_weight.shape, jnp.bfloat16),
            exchange,
            exchange,
            exchange,
            pltpu.VMEM((rows, cols), jnp.bfloat16),
            pltpu.VMEM((devices, 2 * BLOCK, HEAD_DIM), jnp.bfloat16),
            pltpu.VMEM((KV_HEADS, rows, HEAD_DIM), jnp.float32),
            pltpu.VMEM((devices, rows, HEAD_DIM), jnp.float32),
            pltpu.VMEM((devices, rows * cols // HEAD_DIM, BLOCK), jnp.float32),
            wide_half,
            wide_half,
            wide_half,
            wide_half,
            half,
            half,
            pltpu.VMEM((rows, cols), jnp.float32),
            dma((5,)),
            dma((3,)),
            *([dma((chips,)), dma((devices,)), dma((chips,))] * 4),
            *([dma((chips,))] * 8),
        ],
        compiler_params=pltpu.CompilerParams(
            collective_id=0, has_side_effects=True, vmem_limit_bytes=67043328
        ),
    )(
        x_rows,
        attn_gain,
        q_weight,
        o_weight,
        mlp_gain,
        gate_weight,
        up_weight,
        down_weight,
        kv_cache,
        block_mask[:, :, 0],
    )


def solution(mesh):
    fused = mesh.shape["seq"] == 2 * KV_HEADS
    return jax.shard_map(
        layer if fused else local,
        mesh=mesh,
        in_specs=(
            P("group", "seq"),
            P(),
            P(None, "seq"),
            P("seq", None),
            P(),
            P(None, "seq"),
            P(None, "seq"),
            P("seq", None),
            P(None, ("group", "seq"), None),
            P("group", None, "seq"),
        ),
        out_specs=P("group", "seq"),
        check_vma=False,
    )
```

```python
import functools

import jax
import jax.numpy as jnp
from jax import lax
from jax.experimental import pallas as pl
from jax.experimental.pallas import tpu as pltpu
from jax.sharding import PartitionSpec as P

HEADS = 64
KV_HEADS = 8
HEAD_DIM = 128
BLOCK = 128


eps = 1e-05
floor_score = -1e30


def combined_all(x, axis, combine):
    everything = jax.tree.map(lambda part: lax.all_gather(part, axis), x)
    initial = jax.tree.map(lambda part: part[0], everything)

    def turn(k, so_far):
        return combine(so_far, jax.tree.map(lambda part: part[k], everything))

    return lax.fori_loop(1, lax.axis_size(axis), turn, initial)


def rms_norm(values, gain):
    wide = values.astype(jnp.float32)
    inverse = lax.rsqrt(jnp.mean(wide * wide, axis=-1, keepdims=True) + eps)
    return (wide * inverse * gain.astype(jnp.float32)).astype(jnp.bfloat16)


def combine_states(first, second):
    top_a, total_a, accum_a = first
    top_b, total_b, accum_b = second
    top = jnp.maximum(top_a, top_b)
    factor_a = jnp.exp(top_a - top)
    factor_b = jnp.exp(top_b - top)
    return (
        top,
        total_a * factor_a + total_b * factor_b,
        accum_a * factor_a[..., None] + accum_b * factor_b[..., None],
    )


def local(
    x_rows,
    attn_gain,
    q_weight,
    o_weight,
    mlp_gain,
    gate_weight,
    up_weight,
    down_weight,
    kv_cache,
    block_mask,
):
    rows = x_rows.shape[0]
    group = HEADS // KV_HEADS
    key_len = kv_cache.shape[1]
    spans = key_len // BLOCK
    scale = 1.0 / HEAD_DIM**0.5
    whole = lax.all_gather(x_rows, "seq", axis=1, tiled=True)
    normed = rms_norm(whole, attn_gain)
    query_part = jnp.dot(normed, q_weight, preferred_element_type=jnp.float32).astype(jnp.bfloat16)
    queries = lax.all_gather(query_part, "seq", axis=1, tiled=True)
    doc_keys = kv_cache[0]
    doc_values = kv_cache[1]

    def one_group(index):
        query_group = lax.dynamic_slice_in_dim(
            queries, index * (group * HEAD_DIM), group * HEAD_DIM, 1
        ).reshape(rows, group, HEAD_DIM)
        key_group = lax.dynamic_slice_in_dim(doc_keys, index * HEAD_DIM, HEAD_DIM, 1)
        value_group = lax.dynamic_slice_in_dim(doc_values, index * HEAD_DIM, HEAD_DIM, 1)
        mask_group = lax.dynamic_slice_in_dim(block_mask, index, 1, 1)[:, 0, :]
        scores = (
            jnp.einsum("rhd,kd->rhk", query_group, key_group, preferred_element_type=jnp.float32)
            * scale
        )
        scores = scores.reshape(rows, group, spans, BLOCK)
        live = (mask_group == 1)[:, None, :, None]
        masked = jnp.where(live, scores, floor_score)
        local_top = jnp.max(masked, axis=(2, 3))
        weights = jnp.where(live, jnp.exp(masked - local_top[..., None, None]), 0.0)
        local_total = jnp.sum(weights, axis=(2, 3))
        rounded = weights.astype(jnp.bfloat16).reshape(rows, group, key_len)
        local_accum = jnp.einsum(
            "rhk,kd->rhd", rounded, value_group, preferred_element_type=jnp.float32
        )
        return (local_top, local_total, local_accum)

    tops, totals, accums = lax.map(one_group, jnp.arange(KV_HEADS, dtype=jnp.int32))
    local_top = jnp.moveaxis(tops, 0, 1)
    local_total = jnp.moveaxis(totals, 0, 1)
    local_accum = jnp.moveaxis(accums, 0, 1)
    columns = q_weight.shape[1]
    col_start = lax.axis_index("seq") * columns
    top, total, accum = combined_all((local_top, local_total, local_accum), "seq", combine_states)
    attended = accum / total[..., None]
    attended = attended.reshape(rows, HEADS * HEAD_DIM).astype(jnp.bfloat16)
    attn_cols = lax.dynamic_slice_in_dim(attended, col_start, columns, 1)
    weight_cols = o_weight
    attn_out = lax.psum_scatter(
        lax.dot_general(
            weight_cols, attn_cols, (((0,), (1,)), ((), ())), preferred_element_type=jnp.float32
        ),
        "seq",
        scatter_dimension=0,
        tiled=True,
    )
    stream = (x_rows.astype(jnp.float32) + attn_out.T).astype(jnp.bfloat16)
    stream_whole = lax.all_gather(stream, "seq", axis=1, tiled=True)
    normed_two = rms_norm(stream_whole, mlp_gain)
    gate = jnp.dot(normed_two, gate_weight, preferred_element_type=jnp.float32)
    upward = jnp.dot(normed_two, up_weight, preferred_element_type=jnp.float32)
    hidden = (jax.nn.silu(gate) * upward).astype(jnp.bfloat16)
    weight_cols = down_weight
    down_out = lax.psum_scatter(
        lax.dot_general(
            weight_cols, hidden, (((0,), (1,)), ((), ())), preferred_element_type=jnp.float32
        ),
        "seq",
        scatter_dimension=0,
        tiled=True,
    )
    return (stream.astype(jnp.float32) + down_out.T).astype(jnp.bfloat16)


FAR_FIRST = (4, 3, 5, 2, 6, 1, 7)
SCALE = 1.0 / HEAD_DIM**0.5


def layer_kernel(
    x_ref,
    attn_gain,
    q_hbm,
    o_hbm,
    mlp_gain,
    gate_hbm,
    up_hbm,
    down_hbm,
    kv_hbm,
    mask_ref,
    y_ref,
    q_w,
    o_w,
    gate_w,
    up_w,
    down_w,
    x_all,
    s_all,
    normed,
    stream_ref,
    kv_all,
    mask_out,
    mask_all,
    scores,
    pair_out,
    pair_in,
    part_one,
    got_one,
    part_two,
    got_two,
    own_ref,
    w_sem,
    kv_own_sem,
    x_send,
    x_recv,
    x_pass,
    s_send,
    s_recv,
    s_pass,
    kv_send,
    kv_recv,
    kv_pass,
    m_send,
    m_recv,
    m_pass,
    *scatter_sems,
):
    one_sems, two_sems = scatter_sems[:4], scatter_sems[4:]
    devices, rows, cols = x_all.shape
    chips = devices // 2
    group = cols // HEAD_DIM
    me = lax.axis_index("seq")
    chip = me // 2
    core = me % 2
    partner = chip * 2 + 1 - core

    def fetch(k, src, dst):
        return pltpu.make_async_copy(src, dst, w_sem.at[k])

    def remote(src, dst, send, recv, device):
        return pltpu.make_async_remote_copy(
            src_ref=src,
            dst_ref=dst,
            send_sem=send,
            recv_sem=recv,
            device_id={"seq": device},
            device_id_type=pl.DeviceIdType.MESH,
        )

    def chip_at(off):
        return (chip + off) % chips

    def gather_start(src, dst, send, recv):
        for off in FAR_FIRST:
            remote(src, dst.at[me], send.at[off], recv.at[me], chip_at(off) * 2 + core).start()
        remote(src, dst.at[me], send.at[0], recv.at[me], partner).start()

    def gather_pass(dst, send, recv, hand):
        for off in reversed(FAR_FIRST):
            other = chip_at(off) * 2 + core
            remote(dst.at[other], dst.at[other], send.at[off], recv.at[other], partner).wait_recv()
            remote(dst.at[other], dst.at[other], hand.at[off], recv.at[other], partner).start()

    def gather_finish(dst, send, recv):
        for off in range(chips):
            other = chip_at(off) * 2 + 1 - core
            remote(dst.at[other], dst.at[other], send.at[0], recv.at[other], partner).wait_recv()

    def gather_drain(src, dst, send, recv, hand):
        for off in range(chips):
            remote(src, dst.at[me], send.at[off], recv.at[me], partner).wait_send()
        for off in FAR_FIRST:
            remote(src, dst.at[me], hand.at[off], recv.at[me], partner).wait_send()

    fetch_q = fetch(0, q_hbm, q_w)
    fetch_o = fetch(1, o_hbm, o_w)
    fetch_gate = fetch(2, gate_hbm, gate_w)
    fetch_up = fetch(3, up_hbm, up_w)
    fetch_down = fetch(4, down_hbm, down_w)

    barrier = pltpu.get_barrier_semaphore()
    for off in range(1, devices):
        pl.semaphore_signal(
            barrier,
            inc=1,
            device_id={"seq": (me + off) % devices},
            device_id_type=pl.DeviceIdType.MESH,
        )
    fetch_q.start()
    own_kv = pltpu.make_async_copy(
        kv_hbm.at[:, :, pl.ds(pl.multiple_of(chip * HEAD_DIM, HEAD_DIM), HEAD_DIM)],
        kv_all.at[me],
        kv_own_sem,
    )
    own_kv.start()
    fetch_o.start()
    for g in range(KV_HEADS):
        mask_out[g] = jnp.broadcast_to(
            mask_ref[:, g : g + 1].astype(jnp.float32), (rows, HEAD_DIM)
        ).astype(jnp.bfloat16)
    mask_all[me] = mask_out[chip]
    x_all[me] = x_ref[...]
    pl.semaphore_wait(barrier, devices - 1)

    gather_start(x_ref, x_all, x_send, x_recv)

    def kv_of(where):
        return kv_hbm.at[:, :, pl.ds(pl.multiple_of(where * HEAD_DIM, HEAD_DIM), HEAD_DIM)]

    for off in FAR_FIRST:
        there = chip_at(off)
        to = there * 2 + core
        remote(kv_of(there), kv_all.at[me], kv_send.at[off], kv_recv.at[me], to).start()
        remote(mask_out.at[there], mask_all.at[me], m_send.at[off], m_recv.at[me], to).start()
    remote(kv_of(chip), kv_all.at[me], kv_send.at[0], kv_recv.at[me], partner).start()
    remote(mask_out.at[chip], mask_all.at[me], m_send.at[0], m_recv.at[me], partner).start()
    fetch_gate.start()
    fetch_up.start()
    fetch_down.start()

    def norm(values, gain):
        squares = jnp.zeros((rows, cols), jnp.float32)
        for i in range(devices):
            wide = values[i].astype(jnp.float32)
            squares = squares + wide * wide
        mean = jnp.sum(squares, axis=-1, keepdims=True) * (1.0 / (devices * cols))
        inverse = lax.rsqrt(mean + eps)
        for i in range(devices):
            part_gain = gain[i * cols : (i + 1) * cols].astype(jnp.float32).reshape(1, cols)
            normed[i] = (values[i].astype(jnp.float32) * inverse * part_gain).astype(jnp.bfloat16)

    gather_pass(x_all, x_send, x_recv, x_pass)
    gather_finish(x_all, x_send, x_recv)
    norm(x_all, attn_gain)
    fetch_q.wait()
    step = 4

    def q_step(t, total):
        for u in range(step):
            i = t * step + u
            total = total + jnp.dot(
                normed[i],
                q_w[pl.ds(pl.multiple_of(i * cols, cols), cols), :],
                preferred_element_type=jnp.float32,
            )
        return total

    queries = lax.fori_loop(
        0, devices // step, q_step, jnp.zeros((rows, cols), jnp.float32)
    ).astype(jnp.bfloat16)
    query = jnp.concatenate(
        [queries[:, h * HEAD_DIM : (h + 1) * HEAD_DIM] for h in range(group)], axis=0
    )

    gather_pass(kv_all, kv_send, kv_recv, kv_pass)
    gather_pass(mask_all, m_send, m_recv, m_pass)
    own_kv.wait()
    gather_finish(kv_all, kv_send, kv_recv)
    gather_finish(mask_all, m_send, m_recv)

    def live_at(c):
        return jnp.concatenate([mask_all[c].astype(jnp.float32)] * group, axis=0) > 0.5

    tops = []
    for c in range(devices):
        score = (
            lax.dot_general(
                query,
                kv_all[c, 0],
                (((1,), (1,)), ((), ())),
                preferred_element_type=jnp.float32,
            )
            * SCALE
        )
        masked = jnp.where(live_at(c), score, floor_score)
        scores[c] = masked
        tops.append(jnp.max(masked, axis=-1, keepdims=True))
    top = functools.reduce(jnp.maximum, tops)
    total = jnp.zeros((group * rows, 1), jnp.float32)
    accum = jnp.zeros((group * rows, HEAD_DIM), jnp.float32)
    for c in range(devices):
        weight = jnp.where(live_at(c), jnp.exp(scores[c] - tops[c]), 0.0)
        factor = jnp.exp(tops[c] - top)
        total = total + factor * jnp.sum(weight, axis=-1, keepdims=True)
        accum = accum + factor * jnp.dot(
            weight.astype(jnp.bfloat16), kv_all[c, 1], preferred_element_type=jnp.float32
        )
    ratio = accum / total
    attended = jnp.concatenate(
        [ratio[h * rows : (h + 1) * rows] for h in range(group)], axis=1
    ).astype(jnp.bfloat16)

    def scatter(values, weight, pair_out, pair_in, part, got, sems):
        pair_send, pair_recv, send, recv = sems

        def chip_of(s):
            off = chips // 2 + ((s + 1) // 2) * (1 - 2 * (s % 2))
            return chip_at(off)

        def product(where, half):
            to = where * 2 + half
            return jnp.dot(
                values,
                weight[:, pl.ds(pl.multiple_of(to * cols, cols), cols)],
                preferred_element_type=jnp.float32,
            )

        def to_partner(s):
            to = chip_of(s)
            return remote(pair_out.at[to], pair_in.at[to], pair_send.at[s], pair_recv.at[to], partner)

        def to_chip(s):
            to = chip_of(s)
            return remote(part.at[to], got.at[chip], send.at[s], recv.at[chip], to * 2 + core)

        def pair_turn(t, _):
            first = product(chip_of(2 * t), 1 - core)
            second = product(chip_of(2 * t + 1), 1 - core)
            pair_out[chip_of(2 * t)] = first
            pair_out[chip_of(2 * t + 1)] = second

            @pl.when(t > 0)
            def _():
                to_partner(2 * t - 2).start()
                to_partner(2 * t - 1).start()

            return 0

        lax.fori_loop(0, chips // 2, pair_turn, 0)

        def chip_turn(t, _):
            one, two = chip_of(2 * t), chip_of(2 * t + 1)
            first = product(one, core)
            second = product(two, core)

            @pl.when(t == 0)
            def _():
                to_partner(chips - 2).start()
                to_partner(chips - 1).start()

            to_partner(2 * t).wait_recv()
            to_partner(2 * t + 1).wait_recv()
            second = second + pair_in[two]
            part[one] = (first + pair_in[one]).astype(part.dtype)
            part[two] = second.astype(part.dtype)
            own_ref[...] = second

            @pl.when(t > 0)
            def _():
                to_chip(2 * t - 2).start()
                to_chip(2 * t - 1).start()

            return 0

        lax.fori_loop(0, chips // 2, chip_turn, 0)
        to_chip(chips - 2).start()
        total = own_ref[...]
        for off in reversed(FAR_FIRST):
            other = chip_at(off)
            remote(part.at[other], got.at[other], send.at[0], recv.at[other], partner).wait_recv()
            total = total + got[other].astype(jnp.float32)
        for s in range(chips):
            to_partner(s).wait_send()
        return total

    def scatter_drain(part, got, sems):
        _, _, send, recv = sems
        for s in range(chips - 1):
            remote(part.at[0], got.at[chip], send.at[s], recv.at[chip], partner).wait_send()

    fetch_o.wait()
    attn_out = scatter(attended, o_w, pair_out, pair_in, part_one, got_one, one_sems)
    stream = (x_ref[...].astype(jnp.float32) + attn_out).astype(jnp.bfloat16)
    stream_ref[...] = stream
    s_all[me] = stream
    gather_start(stream_ref, s_all, s_send, s_recv)
    gather_pass(s_all, s_send, s_recv, s_pass)
    gather_finish(s_all, s_send, s_recv)
    norm(s_all, mlp_gain)
    fetch_gate.wait()
    fetch_up.wait()
    wide = gate_w.shape[1]

    def ff_step(t, sums):
        gate, upward = sums
        for u in range(2):
            i = t * 2 + u
            at = pl.ds(pl.multiple_of(i * cols, cols), cols)
            gate = gate + jnp.dot(normed[i], gate_w[at, :], preferred_element_type=jnp.float32)
            upward = upward + jnp.dot(normed[i], up_w[at, :], preferred_element_type=jnp.float32)
        return gate, upward

    zeros = jnp.zeros((rows, wide), jnp.float32)
    gate, upward = lax.fori_loop(0, devices // 2, ff_step, (zeros, zeros))
    hidden = (gate / (1.0 + jnp.exp(-gate)) * upward).astype(jnp.bfloat16)
    fetch_down.wait()
    down_out = scatter(hidden, down_w, pair_out, pair_in, part_two, got_two, two_sems)
    y_ref[...] = (stream_ref[...].astype(jnp.float32) + down_out).astype(jnp.bfloat16)

    gather_drain(x_ref, x_all, x_send, x_recv, x_pass)
    gather_drain(kv_of(chip), kv_all, kv_send, kv_recv, kv_pass)
    gather_drain(mask_out.at[0], mask_all, m_send, m_recv, m_pass)
    gather_drain(stream_ref, s_all, s_send, s_recv, s_pass)
    scatter_drain(part_one, got_one, one_sems)
    scatter_drain(part_two, got_two, two_sems)


def layer(
    x_rows,
    attn_gain,
    q_weight,
    o_weight,
    mlp_gain,
    gate_weight,
    up_weight,
    down_weight,
    kv_cache,
    block_mask,
):
    rows, cols = x_rows.shape
    devices = lax.axis_size("seq")
    chips = devices // 2
    wide = gate_weight.shape[1]
    dma = pltpu.SemaphoreType.DMA
    held = pl.BlockSpec(memory_space=pltpu.VMEM)
    left = pl.BlockSpec(memory_space=pl.ANY)
    half = pltpu.VMEM((chips, rows, cols), jnp.bfloat16)
    wide_half = pltpu.VMEM((chips, rows, cols), jnp.float32)
    exchange = pltpu.VMEM((devices, rows, cols), jnp.bfloat16)
    return pl.pallas_call(
        layer_kernel,
        name="layer",
        out_shape=jax.ShapeDtypeStruct((rows, cols), jnp.bfloat16),
        in_specs=[held, held, left, left, held, left, left, left, left, held],
        out_specs=held,
        scratch_shapes=[
            pltpu.VMEM(q_weight.shape, jnp.bfloat16),
            pltpu.VMEM(o_weight.shape, jnp.bfloat16),
            pltpu.VMEM(gate_weight.shape, jnp.bfloat16),
            pltpu.VMEM(up_weight.shape, jnp.bfloat16),
            pltpu.VMEM(down_weight.shape, jnp.bfloat16),
            exchange,
            exchange,
            exchange,
            pltpu.VMEM((rows, cols), jnp.bfloat16),
            pltpu.VMEM((devices, 2, BLOCK, HEAD_DIM), jnp.bfloat16),
            pltpu.VMEM((KV_HEADS, rows, HEAD_DIM), jnp.bfloat16),
            pltpu.VMEM((devices, rows, HEAD_DIM), jnp.bfloat16),
            pltpu.VMEM((devices, rows * cols // HEAD_DIM, BLOCK), jnp.float32),
            wide_half,
            wide_half,
            wide_half,
            wide_half,
            half,
            half,
            pltpu.VMEM((rows, cols), jnp.float32),
            dma((5,)),
            dma(()),
            *([dma((chips,)), dma((devices,)), dma((chips,))] * 4),
            *([dma((chips,))] * 8),
        ],
        compiler_params=pltpu.CompilerParams(
            collective_id=0, has_side_effects=True, vmem_limit_bytes=67043328
        ),
    )(
        x_rows,
        attn_gain,
        q_weight,
        o_weight,
        mlp_gain,
        gate_weight,
        up_weight,
        down_weight,
        kv_cache,
        block_mask[:, :, 0],
    )


def solution(mesh):
    fused = mesh.shape["seq"] == 2 * KV_HEADS
    return jax.shard_map(
        layer if fused else local,
        mesh=mesh,
        in_specs=(
            P("group", "seq"),
            P(),
            P(None, "seq"),
            P("seq", None),
            P(),
            P(None, "seq"),
            P(None, "seq"),
            P("seq", None),
            P(None, ("group", "seq"), None),
            P("group", None, "seq"),
        ),
        out_specs=P("group", "seq"),
        check_vma=False,
    )
```
